32 devices in a mesh: cell: 4 (over y, x), sub: 8 (over z, core).
Axes of the slice: x: 2, y: 2, z: 4, core: 2. Of those that a mesh axis runs over, the one named last changes fastest.
Arguments:
- shell_conc: float32 [4, 32, 10, 128, 128], P('cell', 'sub'), may hold values from 0.2 to 0.8
- heat_rise: float32 [4, 30, 128, 128], P('cell', None, 'sub'), may hold values from -5 to 5
- layer_current: float32 [4, 32, 128, 128], P('cell', 'sub'), may hold values from -4 to 4
- layer_counts: int32 [8], replicated, may hold values from 1 to 4, 30 in all
- contacts: int32 [4, 2], replicated, may hold values from -1 to 3, as said below
Outputs:
- conc_new: float32 [4, 32, 10, 128, 128], P('cell', 'sub')
- heat_new: float32 [4, 30, 128, 128], P('cell', None, 'sub')
The draws below stay inside these ranges and needn't reach their ends.
Inputs may be any that keep to these rules, and one draw needn't show every extreme that they name: `layer_counts`: entry d is the number of consecutive layers held by index d of sub, in order; the entries sum to 30 and the largest is exactly 4. `contacts`: row c names the cell below and the cell above cell c in one stacking order of all 4 cells, each cell once; -1 marks the two ends of the stack.
All inputs are finite; a program needn't handle non-finite values.
Results may differ from the reference program's by a relative error of at most 0.0003.
Values sent between devices are 32-bit elements; how exact they have to be, the bound alone decides.
A program may use at most 64 MiB of HBM per device.

```python
import math
import jax
import jax.numpy as jnp
import numpy as np
from jax import lax

LAYERS = 30
LSLOT = 4
SHELLS = 10
GX = 128
CELLS = 4
SUBS = 8
SLOTS = 32
GY = 128


def draw_contacts(key, part):
    stacking = jax.random.permutation(jax.random.fold_in(key, 11), CELLS).astype(jnp.int32)
    placing = jnp.zeros((CELLS,), jnp.int32).at[stacking].set(jnp.arange(CELLS, dtype=jnp.int32))
    padded = jnp.concatenate([jnp.full((1,), -1, jnp.int32), stacking, jnp.full((1,), -1, jnp.int32)])
    below_cell = padded[placing]
    above_cell = padded[placing + 2]
    return jnp.stack([below_cell, above_cell], axis=1).astype(jnp.int32)


def block_scale(stream_key, extent, shards, low, largest):
    factor_of = 1.0
    for dim, parts in shards:
        steps = jax.random.uniform(jax.random.fold_in(jax.random.fold_in(stream_key, 6), dim), (parts,), jnp.float32, low / len(shards), largest / len(shards))
        factor_of = factor_of * jnp.repeat(jnp.exp(steps), extent[dim] // parts).reshape((-1,) + (1,) * (len(extent) - 1 - dim))
    return factor_of


def length_profile(amount, total, bound, lean):
    weights = [(1 << 20) // math.isqrt(grade ** lean) + 1 for grade in range(2, amount + 1)]
    surplus, given = total - bound - (amount - 1), [1] * (amount - 1)
    while surplus > 0:
        candidates = [i for i in range(amount - 1) if given[i] < bound]
        pool, left = sum([weights[i] for i in candidates]), surplus
        for i in candidates:
            addition = min(bound - given[i], max(1, left * weights[i] // pool), surplus)
            given[i] = given[i] + addition
            surplus = surplus - addition
    return np.array([bound] + given)


def ragged_sizes(key, count, total, bound, slope):
    if count == 2:
        one = jax.random.randint(key, (), max(1, total - bound), min(bound, total - 1) + 1)
        return jnp.stack([one, total - one])
    lengths = jnp.asarray(length_profile(count, total, bound, slope), jnp.int32)
    twos = (count - 1) // 2
    source_of, sink = lengths[1:1 + 2 * twos:2], lengths[2:2 + 2 * twos:2]
    room = jnp.minimum(source_of - 1, bound - sink)
    moved = jax.random.randint(jax.random.fold_in(key, 1), (twos,), 0, 1 << 20) % (room + 1)
    lengths = lengths.at[1:1 + 2 * twos:2].set(source_of - moved).at[2:2 + 2 * twos:2].set(sink + moved)
    return lengths[jax.random.permutation(jax.random.fold_in(key, 2), count)]


def centred(stream_key, shape, scale, reach, cuts=(), kind=jnp.bfloat16):
    drawn = scale * jax.random.normal(stream_key, shape, jnp.float32)
    if cuts:
        drawn = drawn * block_scale(stream_key, shape, cuts, -0.22, 0.18)
    return jnp.clip(drawn, -reach, reach).astype(kind)


def setup_inputs(seed: int = 0) -> dict:
    key_of = jax.random.split(jax.random.key(seed), 6)
    return {
        "shell_conc": jnp.clip(0.2 + 0.6 * jax.random.uniform(key_of[0], (CELLS, SLOTS, SHELLS, GY, GX), jnp.float32) ** block_scale(key_of[0], (CELLS, SLOTS, SHELLS, GY, GX), ((0, 4), (1, 8)), -0.2, 0.2), 0.2, 0.8),
        "heat_rise": jnp.clip(jax.random.uniform(key_of[1], (CELLS, LAYERS, GY, GX), jnp.float32, -5.0, 5.0) * block_scale(key_of[1], (CELLS, LAYERS, GY, GX), ((0, 4), (2, 8)), -0.4, 0.0), -5.0, 5.0),
        "layer_current": centred(key_of[2], (CELLS, SLOTS, GY, GX), 1.0, 4.0, ((0, 4), (1, 8)), jnp.float32),
        "layer_counts": ragged_sizes(key_of[3], SUBS, LAYERS, LSLOT, 2).astype(jnp.int32),
        "contacts": draw_contacts(jax.random.fold_in(key_of[5], 71), 0),
    }


BASE_KELVIN = 298.15
RATE_ACTIVATION = 5000.0
DIFFUSION_ACTIVATION = 3000.0
RATE_CONSTANT = 0.5
VOLT_PER_KELVIN = 2.0 * 8.314462618 / 96485.33212
HEAT_SCALE = 10.0
ENTROPY_SLOPE = 0.001
DIFFUSION_STEP = 0.005
SURFACE_STEP = 0.005
INPLANE_CONDUCT = 0.25
THROUGH_CONDUCT = 2.0
CONTACT_CONDUCT = 0.5

def inverse_sine(value):
    magnitude = jnp.abs(value)
    rooted = jnp.sqrt(1.0 + magnitude * magnitude)
    positive = jnp.log1p(magnitude + magnitude * magnitude / (1.0 + rooted))
    return jnp.where(value < 0.0, -positive, positive)

def layer_tables(layer_counts, slot_count, layer_total):
    counts = layer_counts.astype(jnp.int32)
    finish = jnp.cumsum(counts).astype(jnp.int32)
    starts = (finish - counts).astype(jnp.int32)
    devices = counts.shape[0]
    device_ids = jnp.arange(devices, dtype=jnp.int32)
    slot_index = jnp.arange(devices * slot_count, dtype=jnp.int32)
    slot_owner = slot_index // slot_count
    slot_place = slot_index % slot_count
    owner_hits = slot_owner[:, None] == device_ids[None, :]
    owner_count = lax.optimization_barrier(jnp.sum(jnp.where(owner_hits, counts[None, :], 0), axis=1)).astype(jnp.int32)
    owner_start = lax.optimization_barrier(jnp.sum(jnp.where(owner_hits, starts[None, :], 0), axis=1)).astype(jnp.int32)
    live_slot = slot_place < owner_count
    slot_layer = jnp.minimum(owner_start + slot_place, layer_total - 1).astype(jnp.int32)
    layer_index = jnp.arange(layer_total, dtype=jnp.int32)
    layer_owner = lax.optimization_barrier(jnp.sum((finish[None, :] <= layer_index[:, None]).astype(jnp.int32), axis=1)).astype(jnp.int32)
    layer_hits = layer_owner[:, None] == device_ids[None, :]
    layer_start = lax.optimization_barrier(jnp.sum(jnp.where(layer_hits, starts[None, :], 0), axis=1)).astype(jnp.int32)
    layer_slot = (layer_owner * slot_count + layer_index - layer_start).astype(jnp.int32)
    return (live_slot, slot_layer, layer_slot)

def kinetics(surface, kelvin, current):
    reciprocal = 1.0 / BASE_KELVIN - 1.0 / kelvin
    base_rate = RATE_CONSTANT * jnp.exp(RATE_ACTIVATION * reciprocal) * jnp.sqrt(surface * (1.0 - surface))
    ratio_rate = current / (2.0 * base_rate)
    arcsine = inverse_sine(ratio_rate)
    overvoltage = VOLT_PER_KELVIN * kelvin * arcsine
    entropic = ENTROPY_SLOPE * (0.5 - surface)
    source = HEAT_SCALE * current * (overvoltage + kelvin * entropic)
    heat_slope = HEAT_SCALE * current * (VOLT_PER_KELVIN * arcsine - VOLT_PER_KELVIN * ratio_rate * RATE_ACTIVATION / (kelvin * jnp.sqrt(1.0 + ratio_rate * ratio_rate)) + entropic)
    return (source, heat_slope)

def particle(states, kelvin, current):
    shells = states.shape[1]
    speedup = jnp.exp(DIFFUSION_ACTIVATION * (1.0 / BASE_KELVIN - 1.0 / kelvin))
    volumes = [((radial + 1) ** 3 - radial ** 3) / (3.0 * shells ** 3) for radial in range(shells)]
    linkage = [DIFFUSION_STEP * speedup * ((radial + 1) ** 2 / shells ** 2 * shells) for radial in range(shells - 1)]
    uppers = []
    values = []
    for radial in range(shells):
        diagonal = volumes[radial] + jnp.zeros_like(kelvin)
        right_side = volumes[radial] * states[:, radial]
        if radial < shells - 1:
            diagonal = diagonal + linkage[radial]
        else:
            right_side = right_side - SURFACE_STEP * current
        if radial > 0:
            diagonal = diagonal + linkage[radial - 1] - linkage[radial - 1] * uppers[radial - 1]
            right_side = right_side + linkage[radial - 1] * values[radial - 1]
        if radial < shells - 1:
            uppers.append(linkage[radial] / diagonal)
        else:
            uppers.append(jnp.zeros_like(kelvin))
        values.append(right_side / diagonal)
    result = [None] * shells
    result[shells - 1] = values[shells - 1]
    for radial in range(shells - 2, -1, -1):
        result[radial] = values[radial] + uppers[radial] * result[radial + 1]
    return jnp.stack(result, axis=1)

def column_solve(right_side, heat_slope):
    layer_total = right_side.shape[1]
    uppers = []
    values = []
    for height in range(layer_total):
        diagonal = 1.0 - heat_slope[:, height]
        source = right_side[:, height]
        if height > 0:
            diagonal = diagonal + THROUGH_CONDUCT - THROUGH_CONDUCT * uppers[height - 1]
            source = source + THROUGH_CONDUCT * values[height - 1]
        if height < layer_total - 1:
            diagonal = diagonal + THROUGH_CONDUCT
        uppers.append(THROUGH_CONDUCT / diagonal)
        values.append(source / diagonal)
    result = [None] * layer_total
    result[layer_total - 1] = values[layer_total - 1]
    for height in range(layer_total - 2, -1, -1):
        result[height] = values[height] + uppers[height] * result[height + 1]
    return jnp.stack(result, axis=1)

def reference(shell_conc, heat_rise, layer_current, layer_counts, contacts):
    live_slot, slot_layer, layer_slot = layer_tables(layer_counts, LSLOT, LAYERS)
    slot_rise = jnp.take(heat_rise, slot_layer, axis=1)
    kelvin = BASE_KELVIN + slot_rise
    surface = shell_conc[:, :, SHELLS - 1]
    source, heat_slope = kinetics(surface, kelvin, layer_current)

    def per_cell(operands):
        return particle(operands[0], operands[1], operands[2])
    updated = lax.map(per_cell, (shell_conc, kelvin, layer_current))
    conc_new = jnp.where(live_slot[None, :, None, None, None], updated, 0.0)
    layer_source = jnp.take(source, layer_slot, axis=1)
    layer_slope = jnp.take(heat_slope, layer_slot, axis=1)
    lower_cell = contacts[:, 0]
    upper_cell = contacts[:, 1]
    below_face = jnp.where((lower_cell >= 0)[:, None, None], jnp.take(heat_rise[:, LAYERS - 1], jnp.maximum(lower_cell, 0), axis=0), 0.0)
    above_face = jnp.where((upper_cell >= 0)[:, None, None], jnp.take(heat_rise[:, 0], jnp.maximum(upper_cell, 0), axis=0), 0.0)
    padded = jnp.pad(heat_rise, ((0, 0), (0, 0), (1, 1), (1, 1)), mode='edge')
    laplace = padded[:, :, 2:, 1:-1] + padded[:, :, :-2, 1:-1] + padded[:, :, 1:-1, 2:] + padded[:, :, 1:-1, :-2] - 4.0 * heat_rise
    right_side = heat_rise + INPLANE_CONDUCT * laplace + layer_source - layer_slope * heat_rise
    first_row = right_side[:, 0] + CONTACT_CONDUCT * (below_face - heat_rise[:, 0])
    last_row = right_side[:, LAYERS - 1] + CONTACT_CONDUCT * (above_face - heat_rise[:, LAYERS - 1])
    right_side = jnp.concatenate([first_row[:, None], right_side[:, 1:LAYERS - 1], last_row[:, None]], axis=1)
    heat_new = column_solve(right_side, layer_slope)
    return (conc_new, heat_new)
```

```python
import functools

import jax
import jax.numpy as jnp
from jax import lax
from jax.experimental import pallas as pl
from jax.experimental.pallas import tpu as pltpu
from jax.sharding import PartitionSpec as P

BASE_KELVIN = 298.15
RATE_ACTIVATION = 5000.0
DIFFUSION_ACTIVATION = 3000.0
RATE_CONSTANT = 0.5
VOLT_PER_KELVIN = 2.0 * 8.314462618 / 96485.33212
HEAT_SCALE = 10.0
ENTROPY_SLOPE = 0.001
DIFFUSION_STEP = 0.005
SURFACE_STEP = 0.005
INPLANE_CONDUCT = 0.25
THROUGH_CONDUCT = 2.0
CONTACT_CONDUCT = 0.5
MESH = pl.DeviceIdType.MESH


def partner(me, offset):
    bit = 1
    result = me
    while bit <= offset:
        if offset & bit:
            result = result + bit * (1 - 2 * ((me // bit) % 2))
        bit *= 2
    return result


def peer_of(me, offset, count):
    if count & (count - 1) == 0:
        return partner(me, offset)
    return (me + offset) % count


def inverse_sine(value):
    magnitude = jnp.abs(value)
    rooted = jnp.sqrt(1.0 + magnitude * magnitude)
    positive = jnp.log1p(magnitude + magnitude * magnitude / (1.0 + rooted))
    return jnp.where(value < 0.0, -positive, positive), rooted


def kinetics(surface, rise, current):
    kelvin = BASE_KELVIN + rise
    per_kelvin = 1.0 / kelvin
    reciprocal = rise * (1.0 / BASE_KELVIN) * per_kelvin
    ratio_rate = (
        current
        * jnp.exp(-RATE_ACTIVATION * reciprocal)
        * lax.rsqrt(surface * (1.0 - surface))
        * (0.5 / RATE_CONSTANT)
    )
    arcsine, rooted = inverse_sine(ratio_rate)
    entropic = ENTROPY_SLOPE * (0.5 - surface)
    scaled = HEAT_SCALE * current
    common = VOLT_PER_KELVIN * arcsine + entropic
    source = scaled * kelvin * common
    heat_slope = scaled * (
        common - (VOLT_PER_KELVIN * RATE_ACTIVATION) * ratio_rate * per_kelvin / rooted
    )
    return source, heat_slope


def kernel(
    cells, subs,
    counts, contacts, heat, conc, current,
    conc_new, heat_new,
    staged, slot_rise, conc_in, current_in, surface_rows, current_rows,
    low_edge, high_edge, faces, base, extra, diagonal, layer_slot,
    own_sem, heat_send, heat_recv, surf_send, surf_recv, curr_send, curr_recv,
    edge_send, edge_recv, face_send, face_recv, out_sem,
):
    cell = lax.axis_index("cell")
    sub = lax.axis_index("sub")
    slots, shells, gy, gx = conc_in.shape
    layers, rows, _ = heat.shape[1:]

    offsets = list(range(1, subs))
    far_first = offsets[::-1]

    def at_sub(index):
        return (cell, index)

    barrier = pltpu.get_barrier_semaphore()
    for offset in offsets:
        pl.semaphore_signal(
            barrier, inc=1, device_id=at_sub(peer_of(sub, offset, subs)), device_id_type=MESH
        )
    for offset in range(1, cells):
        pl.semaphore_signal(
            barrier, inc=1, device_id=(peer_of(cell, offset, cells), sub), device_id_type=MESH
        )

    loads = [
        pltpu.make_async_copy(current.at[0], current_in, own_sem.at[0]),
        pltpu.make_async_copy(conc.at[0], conc_in, own_sem.at[1]),
    ]
    for load in loads:
        load.start()

    start = jnp.int32(0)
    for index in range(subs):
        held = counts[index]
        for place in range(slots):
            layer = jnp.minimum(start + place, layers - 1)
            staged[index * slots + place] = heat[0, layer]
        start = start + held
    faces[cell] = jnp.zeros((2, rows, gx), jnp.float32)

    def slot_of(layer, carry):
        total = jnp.int32(0)
        slot = layer
        for index in range(subs):
            total = total + counts[index]
            slot = slot + jnp.where(total <= layer, slots - counts[index], 0)
        layer_slot[layer] = jnp.minimum(slot, subs * slots - 1)
        return carry

    pl.semaphore_wait(barrier, subs - 1 + cells - 1)

    sends = []

    def rows_of(index):
        return pl.ds(pl.multiple_of(index * rows, rows), rows)

    def slots_of(index):
        return pl.ds(index * slots, slots)

    def heat_copy(source, target, device):
        return pltpu.make_async_remote_copy(
            src_ref=staged.at[slots_of(target)],
            dst_ref=slot_rise.at[:, rows_of(source)],
            send_sem=heat_send.at[target],
            recv_sem=heat_recv.at[source],
            device_id=at_sub(device),
            device_id_type=MESH,
        )

    def surf_copy(source, target, device):
        return pltpu.make_async_remote_copy(
            src_ref=conc.at[0, :, shells - 1, rows_of(target)],
            dst_ref=surface_rows.at[slots_of(source)],
            send_sem=surf_send.at[target],
            recv_sem=surf_recv.at[source],
            device_id=at_sub(device),
            device_id_type=MESH,
        )

    def curr_copy(source, target, device):
        return pltpu.make_async_remote_copy(
            src_ref=current.at[0, :, rows_of(target)],
            dst_ref=current_rows.at[slots_of(source)],
            send_sem=curr_send.at[target],
            recv_sem=curr_recv.at[source],
            device_id=at_sub(device),
            device_id_type=MESH,
        )

    for offset in far_first:
        other = peer_of(sub, offset, subs)
        copy = heat_copy(sub, other, other)
        copy.start()
        sends.append(copy)

    to_below = pltpu.make_async_remote_copy(
        src_ref=heat.at[0, :, pl.ds(0, 1)],
        dst_ref=high_edge,
        send_sem=edge_send.at[0],
        recv_sem=edge_recv.at[0],
        device_id=at_sub(jnp.maximum(sub - 1, 0)),
        device_id_type=MESH,
    )
    to_above = pltpu.make_async_remote_copy(
        src_ref=heat.at[0, :, pl.ds(rows - 1, 1)],
        dst_ref=low_edge,
        send_sem=edge_send.at[1],
        recv_sem=edge_recv.at[1],
        device_id=at_sub(jnp.minimum(sub + 1, subs - 1)),
        device_id_type=MESH,
    )

    @pl.when(sub > 0)
    def _():
        to_below.start()

    @pl.when(sub < subs - 1)
    def _():
        to_above.start()

    def face_copies(source, device):
        return [
            pltpu.make_async_remote_copy(
                src_ref=heat.at[0, layer],
                dst_ref=faces.at[source, place],
                send_sem=face_send.at[2 * device + place],
                recv_sem=face_recv.at[2 * source + place],
                device_id=(device, sub),
                device_id_type=MESH,
            )
            for place, layer in ((0, 0), (1, layers - 1))
        ]

    for offset in range(1, cells):
        for copy in face_copies(cell, peer_of(cell, offset, cells)):
            copy.start()
            sends.append(copy)

    for offset in far_first:
        other = peer_of(sub, offset, subs)
        for copy in (surf_copy(sub, other, other), curr_copy(sub, other, other)):
            copy.start()
            sends.append(copy)
    mine = [
        pltpu.make_async_copy(
            conc.at[0, :, shells - 1, rows_of(sub)], surface_rows.at[slots_of(sub)], own_sem.at[2]
        ),
        pltpu.make_async_copy(
            current.at[0, :, rows_of(sub)], current_rows.at[slots_of(sub)], own_sem.at[3]
        ),
    ]
    for copy in mine:
        copy.start()
    slot_rise[:, rows_of(sub)] = staged[slots_of(sub)]

    lax.fori_loop(0, layers, slot_of, jnp.int32(0))

    live_count = counts[sub]
    live = lax.broadcasted_iota(jnp.int32, (slots, rows, gx), 0) < live_count
    volumes = [((r + 1) ** 3 - r**3) / (3.0 * shells**3) for r in range(shells)]
    weights = [DIFFUSION_STEP * ((r + 1) ** 2 / shells**2 * shells) for r in range(shells - 1)]

    def particle(where):
        rise = slot_rise[:, where]
        speedup = jnp.exp(
            (DIFFUSION_ACTIVATION / BASE_KELVIN) * rise / (BASE_KELVIN + rise)
        )
        uppers = []
        values = []
        link = None
        for r in range(shells):
            right = volumes[r] * conc_in[:, r, where]
            if r == shells - 1:
                right = right - SURFACE_STEP * current_in[:, where]
            pivot = volumes[r]
            if r > 0:
                pivot = pivot + link * (1.0 - uppers[r - 1])
                right = right + link * values[r - 1]
            if r < shells - 1:
                next_link = weights[r] * speedup
                pivot = pivot + next_link
            inverse = 1.0 / pivot
            if r < shells - 1:
                uppers.append(next_link * inverse)
                link = next_link
            values.append(right * inverse)
        result = values[shells - 1]
        conc_in[:, shells - 1, where] = jnp.where(live, result, 0.0)
        for r in range(shells - 2, -1, -1):
            result = values[r] + uppers[r] * result
            conc_in[:, r, where] = jnp.where(live, result, 0.0)

    def write(index):
        where = rows_of(index)
        return pltpu.make_async_copy(
            conc_in.at[:, :, where], conc_new.at[0, :, :, where], out_sem.at[index]
        )

    for load in loads:
        load.wait()
    for offset in [0] + offsets:
        other = peer_of(sub, offset, subs)
        if offset:
            heat_copy(other, sub, other).wait_recv()
        particle(rows_of(other))
        write(other).start()

    @pl.when(sub > 0)
    def _():
        to_above.wait_recv()

    @pl.when(sub == 0)
    def _():
        low_edge[...] = heat[0, :, pl.ds(0, 1)]

    @pl.when(sub < subs - 1)
    def _():
        to_below.wait_recv()

    @pl.when(sub == subs - 1)
    def _():
        high_edge[...] = heat[0, :, pl.ds(rows - 1, 1)]

    for offset in range(1, cells):
        other = peer_of(cell, offset, cells)
        for copy in face_copies(other, other):
            copy.wait_recv()

    row_index = lax.broadcasted_iota(jnp.int32, (rows, gx), 0)
    lane_index = lax.broadcasted_iota(jnp.int32, (rows, gx), 1)

    def fill(layer, carry):
        here = heat[0, layer]
        up = pltpu.roll(here, 1, 0)
        up = jnp.where(row_index == 0, low_edge[layer], up)
        down = pltpu.roll(here, rows - 1, 0)
        down = jnp.where(row_index == rows - 1, high_edge[layer], down)
        left = jnp.where(lane_index == 0, here, pltpu.roll(here, 1, 1))
        right = jnp.where(lane_index == gx - 1, here, pltpu.roll(here, gx - 1, 1))
        laplace = down + up + right + left - 4.0 * here
        base[layer] = here + INPLANE_CONDUCT * laplace
        return carry

    lax.fori_loop(0, layers, fill, jnp.int32(0), unroll=2)
    lower = contacts[cell, 0]
    upper = contacts[cell, 1]
    below_face = jnp.where(lower >= 0, faces[jnp.maximum(lower, 0), 1], 0.0)
    above_face = jnp.where(upper >= 0, faces[jnp.maximum(upper, 0), 0], 0.0)
    base[0] = base[0] + CONTACT_CONDUCT * (below_face - heat[0, 0])
    base[layers - 1] = base[layers - 1] + CONTACT_CONDUCT * (above_face - heat[0, layers - 1])

    for offset in [0] + offsets:
        other = peer_of(sub, offset, subs)
        if offset:
            surf_copy(other, sub, other).wait_recv()
            curr_copy(other, sub, other).wait_recv()
        else:
            for copy in mine:
                copy.wait()
        at = slots_of(other)
        rise = staged[at]
        source, slope = kinetics(surface_rows[at], rise, current_rows[at])
        extra[at] = source - slope * rise
        diagonal[at] = 1.0 - slope

    def row_of(layer):
        slot = layer_slot[layer]
        ends = (layer > 0) + (layer < layers - 1)
        return diagonal[slot] + ends * THROUGH_CONDUCT, base[layer] + extra[slot]

    def sweep(order):
        factors, values = [], []
        for layer in order:
            pivot, right = row_of(layer)
            if factors:
                pivot = pivot - THROUGH_CONDUCT * factors[-1]
                right = right + THROUGH_CONDUCT * values[-1]
            inverse = 1.0 / pivot
            factors.append(THROUGH_CONDUCT * inverse)
            values.append(right * inverse)
        return factors, values

    middle = layers // 2
    low_f, low_v = sweep(range(middle))
    high_f, high_v = sweep(range(layers - 1, middle - 1, -1))
    low = (low_v[-1] + low_f[-1] * high_v[-1]) / (1.0 - low_f[-1] * high_f[-1])
    high = high_v[-1] + high_f[-1] * low
    heat_new[0, middle - 1] = low
    heat_new[0, middle] = high
    for step in range(middle - 2, -1, -1):
        low = low_v[step] + low_f[step] * low
        heat_new[0, step] = low
    for step in range(len(high_v) - 2, -1, -1):
        high = high_v[step] + high_f[step] * high
        heat_new[0, layers - 1 - step] = high

    for copy in sends:
        copy.wait_send()

    @pl.when(sub > 0)
    def _():
        to_below.wait_send()

    @pl.when(sub < subs - 1)
    def _():
        to_above.wait_send()

    for index in range(subs):
        write(index).wait()


def per_device(cells, subs, shell_conc, heat_rise, layer_current, layer_counts, contacts):
    _, slots, shells, gy, gx = shell_conc.shape
    _, layers, rows, _ = heat_rise.shape
    f32 = jnp.float32
    dma = pltpu.SemaphoreType.DMA
    conc_new, heat_new = pl.pallas_call(
        functools.partial(kernel, cells, subs),
        out_shape=(
            jax.ShapeDtypeStruct(shell_conc.shape, f32),
            jax.ShapeDtypeStruct(heat_rise.shape, f32),
        ),
        in_specs=[
            pl.BlockSpec(memory_space=pltpu.SMEM),
            pl.BlockSpec(memory_space=pltpu.SMEM),
            pl.BlockSpec(memory_space=pltpu.VMEM),
            pl.BlockSpec(memory_space=pl.ANY),
            pl.BlockSpec(memory_space=pl.ANY),
        ],
        out_specs=(
            pl.BlockSpec(memory_space=pl.ANY),
            pl.BlockSpec(memory_space=pltpu.VMEM),
        ),
        scratch_shapes=[
            pltpu.VMEM((subs * slots, rows, gx), f32),
            pltpu.VMEM((slots, gy, gx), f32),
            pltpu.VMEM((slots, shells, gy, gx), f32),
            pltpu.VMEM((slots, gy, gx), f32),
            pltpu.VMEM((subs * slots, rows, gx), f32),
            pltpu.VMEM((subs * slots, rows, gx), f32),
            pltpu.VMEM((layers, 1, gx), f32),
            pltpu.VMEM((layers, 1, gx), f32),
            pltpu.VMEM((cells, 2, rows, gx), f32),
            pltpu.VMEM((layers, rows, gx), f32),
            pltpu.VMEM((subs * slots, rows, gx), f32),
            pltpu.VMEM((subs * slots, rows, gx), f32),
            pltpu.SMEM((layers,), jnp.int32),
            dma((4,)),
            dma((subs,)),
            dma((subs,)),
            dma((subs,)),
            dma((subs,)),
            dma((subs,)),
            dma((subs,)),
            dma((2,)),
            dma((2,)),
            dma((2 * cells,)),
            dma((2 * cells,)),
            dma((subs,)),
        ],
        compiler_params=pltpu.CompilerParams(collective_id=0, has_side_effects=True),
    )(layer_counts, contacts, heat_rise, shell_conc, layer_current)
    return conc_new, heat_new


def solution(mesh):
    in_specs = (
        P("cell", "sub", None, None, None),
        P("cell", None, "sub", None),
        P("cell", "sub", None, None),
        P(),
        P(),
    )
    out_specs = (P("cell", "sub", None, None, None), P("cell", None, "sub", None))
    body = functools.partial(per_device, mesh.shape["cell"], mesh.shape["sub"])
    return jax.shard_map(
        body, mesh=mesh, in_specs=in_specs, out_specs=out_specs, check_vma=False
    )
```

```python
import functools

import jax
import jax.numpy as jnp
from jax import lax
from jax.experimental import pallas as pl
from jax.experimental.pallas import tpu as pltpu
from jax.sharding import PartitionSpec as P

BASE_KELVIN = 298.15
RATE_ACTIVATION = 5000.0
DIFFUSION_ACTIVATION = 3000.0
RATE_CONSTANT = 0.5
VOLT_PER_KELVIN = 2.0 * 8.314462618 / 96485.33212
HEAT_SCALE = 10.0
ENTROPY_SLOPE = 0.001
DIFFUSION_STEP = 0.005
SURFACE_STEP = 0.005
INPLANE_CONDUCT = 0.25
THROUGH_CONDUCT = 2.0
CONTACT_CONDUCT = 0.5
MESH = pl.DeviceIdType.MESH
GRANT = 24 << 20


def partner(me, offset):
    bit = 1
    result = me
    while bit <= offset:
        if offset & bit:
            result = result + bit * (1 - 2 * ((me // bit) % 2))
        bit *= 2
    return result


def peer_of(me, offset, count):
    if count & (count - 1) == 0:
        return partner(me, offset)
    return (me + offset) % count


def inverse_sine(value):
    magnitude = jnp.abs(value)
    rooted = jnp.sqrt(1.0 + magnitude * magnitude)
    positive = jnp.log1p(magnitude + magnitude * magnitude / (1.0 + rooted))
    return jnp.where(value < 0.0, -positive, positive), rooted


def kinetics(surface, rise, current):
    kelvin = BASE_KELVIN + rise
    per_kelvin = 1.0 / kelvin
    reciprocal = rise * (1.0 / BASE_KELVIN) * per_kelvin
    ratio_rate = (
        current
        * jnp.exp(-RATE_ACTIVATION * reciprocal)
        * lax.rsqrt(surface * (1.0 - surface))
        * (0.5 / RATE_CONSTANT)
    )
    arcsine, rooted = inverse_sine(ratio_rate)
    entropic = ENTROPY_SLOPE * (0.5 - surface)
    scaled = HEAT_SCALE * current
    common = VOLT_PER_KELVIN * arcsine + entropic
    source = scaled * kelvin * common
    heat_slope = scaled * (
        common - (VOLT_PER_KELVIN * RATE_ACTIVATION) * ratio_rate * per_kelvin / rooted
    )
    return source, heat_slope


def kernel(
    cells, subs,
    counts, contacts, heat_hbm, conc, current,
    conc_in, right_side, pivots,
    heat, staged, slot_rise, current_in, surface_rows, current_rows,
    low_edge, high_edge, faces, base, extra, diagonal, layer_slot,
    own_sem, heat_send, heat_recv, surf_send, surf_recv, curr_send, curr_recv,
    edge_send, edge_recv, face_send, face_recv,
):
    cell = lax.axis_index("cell")
    sub = lax.axis_index("sub")
    slots, shells, gy, gx = conc_in.shape
    layers, rows, _ = heat.shape[1:]

    offsets = list(range(1, subs))
    far_first = offsets[::-1]

    def at_sub(index):
        return (cell, index)

    heat_load = pltpu.make_async_copy(heat_hbm, heat, own_sem.at[4])
    heat_load.start()
    barrier = pltpu.get_barrier_semaphore()
    for offset in offsets:
        pl.semaphore_signal(
            barrier, inc=1, device_id=at_sub(peer_of(sub, offset, subs)), device_id_type=MESH
        )
    for offset in range(1, cells):
        pl.semaphore_signal(
            barrier, inc=1, device_id=(peer_of(cell, offset, cells), sub), device_id_type=MESH
        )

    loads = [
        pltpu.make_async_copy(current.at[0], current_in, own_sem.at[0]),
        pltpu.make_async_copy(conc.at[0], conc_in, own_sem.at[1]),
    ]
    for load in loads:
        load.start()

    heat_load.wait()
    start = jnp.int32(0)
    for index in range(subs):
        held = counts[index]
        for place in range(slots):
            layer = jnp.minimum(start + place, layers - 1)
            staged[index * slots + place] = heat[0, layer]
        start = start + held
    faces[cell] = jnp.zeros((2, rows, gx), jnp.float32)

    def slot_of(layer, carry):
        total = jnp.int32(0)
        slot = layer
        for index in range(subs):
            total = total + counts[index]
            slot = slot + jnp.where(total <= layer, slots - counts[index], 0)
        layer_slot[layer] = jnp.minimum(slot, subs * slots - 1)
        return carry

    pl.semaphore_wait(barrier, subs - 1 + cells - 1)

    sends = []

    def rows_of(index):
        return pl.ds(pl.multiple_of(index * rows, rows), rows)

    def slots_of(index):
        return pl.ds(index * slots, slots)

    def heat_copy(source, target, device):
        return pltpu.make_async_remote_copy(
            src_ref=staged.at[slots_of(target)],
            dst_ref=slot_rise.at[:, rows_of(source)],
            send_sem=heat_send.at[target],
            recv_sem=heat_recv.at[source],
            device_id=at_sub(device),
            device_id_type=MESH,
        )

    def surf_copy(source, target, device):
        return pltpu.make_async_remote_copy(
            src_ref=conc.at[0, :, shells - 1, rows_of(target)],
            dst_ref=surface_rows.at[slots_of(source)],
            send_sem=surf_send.at[target],
            recv_sem=surf_recv.at[source],
            device_id=at_sub(device),
            device_id_type=MESH,
        )

    def curr_copy(source, target, device):
        return pltpu.make_async_remote_copy(
            src_ref=current.at[0, :, rows_of(target)],
            dst_ref=current_rows.at[slots_of(source)],
            send_sem=curr_send.at[target],
            recv_sem=curr_recv.at[source],
            device_id=at_sub(device),
            device_id_type=MESH,
        )

    for offset in far_first:
        other = peer_of(sub, offset, subs)
        copy = heat_copy(sub, other, other)
        copy.start()
        sends.append(copy)

    to_below = pltpu.make_async_remote_copy(
        src_ref=heat_hbm.at[0, :, pl.ds(0, 1)],
        dst_ref=high_edge,
        send_sem=edge_send.at[0],
        recv_sem=edge_recv.at[0],
        device_id=at_sub(jnp.maximum(sub - 1, 0)),
        device_id_type=MESH,
    )
    to_above = pltpu.make_async_remote_copy(
        src_ref=heat_hbm.at[0, :, pl.ds(rows - 1, 1)],
        dst_ref=low_edge,
        send_sem=edge_send.at[1],
        recv_sem=edge_recv.at[1],
        device_id=at_sub(jnp.minimum(sub + 1, subs - 1)),
        device_id_type=MESH,
    )

    @pl.when(sub > 0)
    def _():
        to_below.start()

    @pl.when(sub < subs - 1)
    def _():
        to_above.start()

    def face_copies(source, device):
        return [
            pltpu.make_async_remote_copy(
                src_ref=heat_hbm.at[0, layer],
                dst_ref=faces.at[source, place],
                send_sem=face_send.at[2 * device + place],
                recv_sem=face_recv.at[2 * source + place],
                device_id=(device, sub),
                device_id_type=MESH,
            )
            for place, layer in ((0, 0), (1, layers - 1))
        ]

    for offset in range(1, cells):
        for copy in face_copies(cell, peer_of(cell, offset, cells)):
            copy.start()
            sends.append(copy)

    for offset in far_first:
        other = peer_of(sub, offset, subs)
        for copy in (surf_copy(sub, other, other), curr_copy(sub, other, other)):
            copy.start()
            sends.append(copy)
    mine = [
        pltpu.make_async_copy(
            conc.at[0, :, shells - 1, rows_of(sub)], surface_rows.at[slots_of(sub)], own_sem.at[2]
        ),
        pltpu.make_async_copy(
            current.at[0, :, rows_of(sub)], current_rows.at[slots_of(sub)], own_sem.at[3]
        ),
    ]
    for copy in mine:
        copy.start()
    slot_rise[:, rows_of(sub)] = staged[slots_of(sub)]

    lax.fori_loop(0, layers, slot_of, jnp.int32(0))

    live_count = counts[sub]
    live = lax.broadcasted_iota(jnp.int32, (slots, rows, gx), 0) < live_count
    volumes = [((r + 1) ** 3 - r**3) / (3.0 * shells**3) for r in range(shells)]
    weights = [DIFFUSION_STEP * ((r + 1) ** 2 / shells**2 * shells) for r in range(shells - 1)]

    def particle(where):
        rise = slot_rise[:, where]
        speedup = jnp.exp(
            (DIFFUSION_ACTIVATION / BASE_KELVIN) * rise / (BASE_KELVIN + rise)
        )
        uppers = []
        values = []
        link = None
        for r in range(shells):
            right = volumes[r] * conc_in[:, r, where]
            if r == shells - 1:
                right = right - SURFACE_STEP * current_in[:, where]
            pivot = volumes[r]
            if r > 0:
                pivot = pivot + link * (1.0 - uppers[r - 1])
                right = right + link * values[r - 1]
            if r < shells - 1:
                next_link = weights[r] * speedup
                pivot = pivot + next_link
            inverse = 1.0 / pivot
            if r < shells - 1:
                uppers.append(next_link * inverse)
                link = next_link
            values.append(right * inverse)
        result = values[shells - 1]
        conc_in[:, shells - 1, where] = jnp.where(live, result, 0.0)
        for r in range(shells - 2, -1, -1):
            result = values[r] + uppers[r] * result
            conc_in[:, r, where] = jnp.where(live, result, 0.0)

    for load in loads:
        load.wait()
    for offset in [0] + offsets:
        other = peer_of(sub, offset, subs)
        if offset:
            heat_copy(other, sub, other).wait_recv()
        particle(rows_of(other))

    @pl.when(sub > 0)
    def _():
        to_above.wait_recv()

    @pl.when(sub == 0)
    def _():
        low_edge[...] = heat[0, :, pl.ds(0, 1)]

    @pl.when(sub < subs - 1)
    def _():
        to_below.wait_recv()

    @pl.when(sub == subs - 1)
    def _():
        high_edge[...] = heat[0, :, pl.ds(rows - 1, 1)]

    for offset in range(1, cells):
        other = peer_of(cell, offset, cells)
        for copy in face_copies(other, other):
            copy.wait_recv()

    row_index = lax.broadcasted_iota(jnp.int32, (rows, gx), 0)
    lane_index = lax.broadcasted_iota(jnp.int32, (rows, gx), 1)

    def fill(layer, carry):
        here = heat[0, layer]
        up = pltpu.roll(here, 1, 0)
        up = jnp.where(row_index == 0, low_edge[layer], up)
        down = pltpu.roll(here, rows - 1, 0)
        down = jnp.where(row_index == rows - 1, high_edge[layer], down)
        left = jnp.where(lane_index == 0, here, pltpu.roll(here, 1, 1))
        right = jnp.where(lane_index == gx - 1, here, pltpu.roll(here, gx - 1, 1))
        laplace = down + up + right + left - 4.0 * here
        base[layer] = here + INPLANE_CONDUCT * laplace
        return carry

    lax.fori_loop(0, layers, fill, jnp.int32(0), unroll=2)
    lower = contacts[0, cell]
    upper = contacts[1, cell]
    below_face = jnp.where(lower >= 0, faces[jnp.maximum(lower, 0), 1], 0.0)
    above_face = jnp.where(upper >= 0, faces[jnp.maximum(upper, 0), 0], 0.0)
    base[0] = base[0] + CONTACT_CONDUCT * (below_face - heat[0, 0])
    base[layers - 1] = base[layers - 1] + CONTACT_CONDUCT * (above_face - heat[0, layers - 1])

    for offset in [0] + offsets:
        other = peer_of(sub, offset, subs)
        if offset:
            surf_copy(other, sub, other).wait_recv()
            curr_copy(other, sub, other).wait_recv()
        else:
            for copy in mine:
                copy.wait()
        at = slots_of(other)
        rise = staged[at]
        source, slope = kinetics(surface_rows[at], rise, current_rows[at])
        extra[at] = source - slope * rise
        diagonal[at] = 1.0 - slope

    for layer in range(layers):
        slot = layer_slot[layer]
        ends = (layer > 0) + (layer < layers - 1)
        pivots[layer] = diagonal[slot] + ends * THROUGH_CONDUCT
        right_side[layer] = base[layer] + extra[slot]

    for copy in sends:
        copy.wait_send()

    @pl.when(sub > 0)
    def _():
        to_below.wait_send()

    @pl.when(sub < subs - 1)
    def _():
        to_above.wait_send()


def finish(conc, right_side, pivots, conc_new, heat_new, sem):
    slots = conc.shape[0]
    layers = right_side.shape[0]
    writes = [
        pltpu.make_async_copy(conc.at[s], conc_new.at[0, s], sem.at[s]) for s in range(slots)
    ]
    for write in writes:
        write.start()

    def sweep(order):
        factors, values = [], []
        for layer in order:
            pivot, right = pivots[layer], right_side[layer]
            if factors:
                pivot = pivot - THROUGH_CONDUCT * factors[-1]
                right = right + THROUGH_CONDUCT * values[-1]
            inverse = 1.0 / pivot
            factors.append(THROUGH_CONDUCT * inverse)
            values.append(right * inverse)
        return factors, values

    middle = layers // 2
    low_f, low_v = sweep(range(middle))
    high_f, high_v = sweep(range(layers - 1, middle - 1, -1))
    low = (low_v[-1] + low_f[-1] * high_v[-1]) / (1.0 - low_f[-1] * high_f[-1])
    high = high_v[-1] + high_f[-1] * low
    heat_new[0, middle - 1] = low
    heat_new[0, middle] = high
    for step in range(middle - 2, -1, -1):
        low = low_v[step] + low_f[step] * low
        heat_new[0, step] = low
    for step in range(len(high_v) - 2, -1, -1):
        high = high_v[step] + high_f[step] * high
        heat_new[0, layers - 1 - step] = high
    for write in writes:
        write.wait()


def per_device(cells, subs, shell_conc, heat_rise, layer_current, layer_counts, contacts):
    _, slots, shells, gy, gx = shell_conc.shape
    _, layers, rows, _ = heat_rise.shape
    f32 = jnp.float32
    dma = pltpu.SemaphoreType.DMA
    table = (layers, rows, gx)
    conc, right_side, pivots = pl.pallas_call(
        functools.partial(kernel, cells, subs),
        out_shape=(
            pltpu.VMEM((slots, shells, gy, gx), f32),
            pltpu.VMEM(table, f32),
            pltpu.VMEM(table, f32),
        ),
        in_specs=[
            pl.BlockSpec(memory_space=pltpu.SMEM),
            pl.BlockSpec(memory_space=pltpu.SMEM),
            pl.BlockSpec(memory_space=pltpu.HBM),
            pl.BlockSpec(memory_space=pltpu.HBM),
            pl.BlockSpec(memory_space=pltpu.HBM),
        ],
        out_specs=(pl.BlockSpec(memory_space=pltpu.VMEM),) * 3,
        scratch_shapes=[
            pltpu.VMEM(heat_rise.shape, f32),
            pltpu.VMEM((subs * slots, rows, gx), f32),
            pltpu.VMEM((slots, gy, gx), f32),
            pltpu.VMEM((slots, gy, gx), f32),
            pltpu.VMEM((subs * slots, rows, gx), f32),
            pltpu.VMEM((subs * slots, rows, gx), f32),
            pltpu.VMEM((layers, 1, gx), f32),
            pltpu.VMEM((layers, 1, gx), f32),
            pltpu.VMEM((cells, 2, rows, gx), f32),
            pltpu.VMEM(table, f32),
            pltpu.VMEM((subs * slots, rows, gx), f32),
            pltpu.VMEM((subs * slots, rows, gx), f32),
            pltpu.SMEM((layers,), jnp.int32),
            dma((5,)),
            dma((subs,)),
            dma((subs,)),
            dma((subs,)),
            dma((subs,)),
            dma((subs,)),
            dma((subs,)),
            dma((2,)),
            dma((2,)),
            dma((2 * cells,)),
            dma((2 * cells,)),
        ],
        compiler_params=pltpu.CompilerParams(
            collective_id=0, has_side_effects=True, vmem_limit_bytes=GRANT
        ),
    )(layer_counts, contacts.T, heat_rise, shell_conc, layer_current)
    conc_new, heat_new = pl.pallas_call(
        finish,
        out_shape=(
            jax.ShapeDtypeStruct(shell_conc.shape, f32),
            jax.ShapeDtypeStruct(heat_rise.shape, f32),
        ),
        in_specs=[pl.BlockSpec(memory_space=pltpu.VMEM)] * 3,
        out_specs=(
            pl.BlockSpec(memory_space=pl.ANY),
            pl.BlockSpec(memory_space=pltpu.VMEM),
        ),
        scratch_shapes=[dma((slots,))],
        compiler_params=pltpu.CompilerParams(vmem_limit_bytes=GRANT),
    )(conc, right_side, pivots)
    return conc_new, heat_new


def solution(mesh):
    in_specs = (
        P("cell", "sub", None, None, None),
        P("cell", None, "sub", None),
        P("cell", "sub", None, None),
        P(),
        P(),
    )
    out_specs = (P("cell", "sub", None, None, None), P("cell", None, "sub", None))
    body = functools.partial(per_device, mesh.shape["cell"], mesh.shape["sub"])
    return jax.shard_map(
        body, mesh=mesh, in_specs=in_specs, out_specs=out_specs, check_vma=False
    )
```

```python
import functools

import jax
import jax.numpy as jnp
from jax import lax
from jax.experimental import pallas as pl
from jax.experimental.pallas import tpu as pltpu
from jax.sharding import PartitionSpec as P

BASE_KELVIN = 298.15
RATE_ACTIVATION = 5000.0
DIFFUSION_ACTIVATION = 3000.0
RATE_CONSTANT = 0.5
VOLT_PER_KELVIN = 2.0 * 8.314462618 / 96485.33212
HEAT_SCALE = 10.0
ENTROPY_SLOPE = 0.001
DIFFUSION_STEP = 0.005
SURFACE_STEP = 0.005
INPLANE_CONDUCT = 0.25
THROUGH_CONDUCT = 2.0
CONTACT_CONDUCT = 0.5
MESH = pl.DeviceIdType.MESH
GRANT = 24 << 20


def partner(me, offset):
    bit = 1
    result = me
    while bit <= offset:
        if offset & bit:
            result = result + bit * (1 - 2 * ((me // bit) % 2))
        bit *= 2
    return result


def peer_of(me, offset, count):
    if count & (count - 1) == 0:
        return partner(me, offset)
    return (me + offset) % count


def inverse_sine(value):
    magnitude = jnp.abs(value)
    rooted = jnp.sqrt(1.0 + magnitude * magnitude)
    positive = jnp.log1p(magnitude + magnitude * magnitude / (1.0 + rooted))
    return jnp.where(value < 0.0, -positive, positive), rooted


def kinetics(surface, rise, current):
    kelvin = BASE_KELVIN + rise
    per_kelvin = 1.0 / kelvin
    reciprocal = rise * (1.0 / BASE_KELVIN) * per_kelvin
    ratio_rate = (
        current
        * jnp.exp(-RATE_ACTIVATION * reciprocal)
        * lax.rsqrt(surface * (1.0 - surface))
        * (0.5 / RATE_CONSTANT)
    )
    arcsine, rooted = inverse_sine(ratio_rate)
    entropic = ENTROPY_SLOPE * (0.5 - surface)
    scaled = HEAT_SCALE * current
    common = VOLT_PER_KELVIN * arcsine + entropic
    source = scaled * kelvin * common
    heat_slope = scaled * (
        common - (VOLT_PER_KELVIN * RATE_ACTIVATION) * ratio_rate * per_kelvin / rooted
    )
    return source, heat_slope


def kernel(
    cells, subs,
    counts_hbm, contacts_hbm, heat_hbm, conc, current,
    conc_in, right_side, pivots,
    heat, staged, slot_rise, current_in, surface_rows, current_rows,
    low_edge, high_edge, faces, base, extra, diagonal, layer_slot, counts, contacts,
    own_sem, heat_send, heat_recv, surf_send, surf_recv, curr_send, curr_recv,
    edge_send, edge_recv, face_send, face_recv,
):
    cell = lax.axis_index("cell")
    sub = lax.axis_index("sub")
    slots, shells, gy, gx = conc_in.shape
    layers, rows, _ = heat.shape[1:]

    offsets = list(range(1, subs))
    far_first = offsets[::-1]

    def at_sub(index):
        return (cell, index)

    first_loads = [
        pltpu.make_async_copy(counts_hbm, counts, own_sem.at[5]),
        pltpu.make_async_copy(heat_hbm, heat, own_sem.at[4]),
        pltpu.make_async_copy(contacts_hbm, contacts, own_sem.at[6]),
    ]
    for load in first_loads:
        load.start()
    barrier = pltpu.get_barrier_semaphore()
    for offset in offsets:
        pl.semaphore_signal(
            barrier, inc=1, device_id=at_sub(peer_of(sub, offset, subs)), device_id_type=MESH
        )
    for offset in range(1, cells):
        pl.semaphore_signal(
            barrier, inc=1, device_id=(peer_of(cell, offset, cells), sub), device_id_type=MESH
        )

    loads = [
        pltpu.make_async_copy(current.at[0], current_in, own_sem.at[0]),
        pltpu.make_async_copy(conc.at[0], conc_in, own_sem.at[1]),
    ]
    for load in loads:
        load.start()

    for load in first_loads:
        load.wait()
    start = jnp.int32(0)
    for index in range(subs):
        held = counts[index]
        for place in range(slots):
            layer = jnp.minimum(start + place, layers - 1)
            staged[index * slots + place] = heat[0, layer]
        start = start + held
    faces[cell] = jnp.zeros((2, rows, gx), jnp.float32)

    def slot_of(layer, carry):
        total = jnp.int32(0)
        slot = layer
        for index in range(subs):
            total = total + counts[index]
            slot = slot + jnp.where(total <= layer, slots - counts[index], 0)
        layer_slot[layer] = jnp.minimum(slot, subs * slots - 1)
        return carry

    pl.semaphore_wait(barrier, subs - 1 + cells - 1)

    sends = []

    def rows_of(index):
        return pl.ds(pl.multiple_of(index * rows, rows), rows)

    def slots_of(index):
        return pl.ds(index * slots, slots)

    def heat_copy(source, target, device):
        return pltpu.make_async_remote_copy(
            src_ref=staged.at[slots_of(target)],
            dst_ref=slot_rise.at[:, rows_of(source)],
            send_sem=heat_send.at[target],
            recv_sem=heat_recv.at[source],
            device_id=at_sub(device),
            device_id_type=MESH,
        )

    def surf_copy(source, target, device):
        return pltpu.make_async_remote_copy(
            src_ref=conc.at[0, :, shells - 1, rows_of(target)],
            dst_ref=surface_rows.at[slots_of(source)],
            send_sem=surf_send.at[target],
            recv_sem=surf_recv.at[source],
            device_id=at_sub(device),
            device_id_type=MESH,
        )

    def curr_copy(source, target, device):
        return pltpu.make_async_remote_copy(
            src_ref=current.at[0, :, rows_of(target)],
            dst_ref=current_rows.at[slots_of(source)],
            send_sem=curr_send.at[target],
            recv_sem=curr_recv.at[source],
            device_id=at_sub(device),
            device_id_type=MESH,
        )

    for offset in far_first:
        other = peer_of(sub, offset, subs)
        copy = heat_copy(sub, other, other)
        copy.start()
        sends.append(copy)

    to_below = pltpu.make_async_remote_copy(
        src_ref=heat_hbm.at[0, :, pl.ds(0, 1)],
        dst_ref=high_edge,
        send_sem=edge_send.at[0],
        recv_sem=edge_recv.at[0],
        device_id=at_sub(jnp.maximum(sub - 1, 0)),
        device_id_type=MESH,
    )
    to_above = pltpu.make_async_remote_copy(
        src_ref=heat_hbm.at[0, :, pl.ds(rows - 1, 1)],
        dst_ref=low_edge,
        send_sem=edge_send.at[1],
        recv_sem=edge_recv.at[1],
        device_id=at_sub(jnp.minimum(sub + 1, subs - 1)),
        device_id_type=MESH,
    )

    @pl.when(sub > 0)
    def _():
        to_below.start()

    @pl.when(sub < subs - 1)
    def _():
        to_above.start()

    def face_copies(source, device):
        return [
            pltpu.make_async_remote_copy(
                src_ref=heat_hbm.at[0, layer],
                dst_ref=faces.at[source, place],
                send_sem=face_send.at[2 * device + place],
                recv_sem=face_recv.at[2 * source + place],
                device_id=(device, sub),
                device_id_type=MESH,
            )
            for place, layer in ((0, 0), (1, layers - 1))
        ]

    for offset in range(1, cells):
        for copy in face_copies(cell, peer_of(cell, offset, cells)):
            copy.start()
            sends.append(copy)

    for offset in far_first:
        other = peer_of(sub, offset, subs)
        for copy in (surf_copy(sub, other, other), curr_copy(sub, other, other)):
            copy.start()
            sends.append(copy)
    mine = [
        pltpu.make_async_copy(
            conc.at[0, :, shells - 1, rows_of(sub)], surface_rows.at[slots_of(sub)], own_sem.at[2]
        ),
        pltpu.make_async_copy(
            current.at[0, :, rows_of(sub)], current_rows.at[slots_of(sub)], own_sem.at[3]
        ),
    ]
    for copy in mine:
        copy.start()
    slot_rise[:, rows_of(sub)] = staged[slots_of(sub)]

    lax.fori_loop(0, layers, slot_of, jnp.int32(0))

    live_count = counts[sub]
    live = lax.broadcasted_iota(jnp.int32, (slots, rows, gx), 0) < live_count
    volumes = [((r + 1) ** 3 - r**3) / (3.0 * shells**3) for r in range(shells)]
    weights = [DIFFUSION_STEP * ((r + 1) ** 2 / shells**2 * shells) for r in range(shells - 1)]

    def particle(where):
        rise = slot_rise[:, where]
        speedup = jnp.exp(
            (DIFFUSION_ACTIVATION / BASE_KELVIN) * rise / (BASE_KELVIN + rise)
        )
        uppers = []
        values = []
        link = None
        for r in range(shells):
            right = volumes[r] * conc_in[:, r, where]
            if r == shells - 1:
                right = right - SURFACE_STEP * current_in[:, where]
            pivot = volumes[r]
            if r > 0:
                pivot = pivot + link * (1.0 - uppers[r - 1])
                right = right + link * values[r - 1]
            if r < shells - 1:
                next_link = weights[r] * speedup
                pivot = pivot + next_link
            inverse = 1.0 / pivot
            if r < shells - 1:
                uppers.append(next_link * inverse)
                link = next_link
            values.append(right * inverse)
        result = values[shells - 1]
        conc_in[:, shells - 1, where] = jnp.where(live, result, 0.0)
        for r in range(shells - 2, -1, -1):
            result = values[r] + uppers[r] * result
            conc_in[:, r, where] = jnp.where(live, result, 0.0)

    for load in loads:
        load.wait()
    for offset in [0] + offsets:
        other = peer_of(sub, offset, subs)
        if offset:
            heat_copy(other, sub, other).wait_recv()
        particle(rows_of(other))

    @pl.when(sub > 0)
    def _():
        to_above.wait_recv()

    @pl.when(sub == 0)
    def _():
        low_edge[...] = heat[0, :, pl.ds(0, 1)]

    @pl.when(sub < subs - 1)
    def _():
        to_below.wait_recv()

    @pl.when(sub == subs - 1)
    def _():
        high_edge[...] = heat[0, :, pl.ds(rows - 1, 1)]

    for offset in range(1, cells):
        other = peer_of(cell, offset, cells)
        for copy in face_copies(other, other):
            copy.wait_recv()

    row_index = lax.broadcasted_iota(jnp.int32, (rows, gx), 0)
    lane_index = lax.broadcasted_iota(jnp.int32, (rows, gx), 1)

    def fill(layer, carry):
        here = heat[0, layer]
        up = pltpu.roll(here, 1, 0)
        up = jnp.where(row_index == 0, low_edge[layer], up)
        down = pltpu.roll(here, rows - 1, 0)
        down = jnp.where(row_index == rows - 1, high_edge[layer], down)
        left = jnp.where(lane_index == 0, here, pltpu.roll(here, 1, 1))
        right = jnp.where(lane_index == gx - 1, here, pltpu.roll(here, gx - 1, 1))
        laplace = down + up + right + left - 4.0 * here
        base[layer] = here + INPLANE_CONDUCT * laplace
        return carry

    lax.fori_loop(0, layers, fill, jnp.int32(0), unroll=2)
    lower = contacts[0, cell]
    upper = contacts[1, cell]
    below_face = jnp.where(lower >= 0, faces[jnp.maximum(lower, 0), 1], 0.0)
    above_face = jnp.where(upper >= 0, faces[jnp.maximum(upper, 0), 0], 0.0)
    base[0] = base[0] + CONTACT_CONDUCT * (below_face - heat[0, 0])
    base[layers - 1] = base[layers - 1] + CONTACT_CONDUCT * (above_face - heat[0, layers - 1])

    for offset in [0] + offsets:
        other = peer_of(sub, offset, subs)
        if offset:
            surf_copy(other, sub, other).wait_recv()
            curr_copy(other, sub, other).wait_recv()
        else:
            for copy in mine:
                copy.wait()
        at = slots_of(other)
        rise = staged[at]
        source, slope = kinetics(surface_rows[at], rise, current_rows[at])
        extra[at] = source - slope * rise
        diagonal[at] = 1.0 - slope

    for layer in range(layers):
        slot = layer_slot[layer]
        ends = (layer > 0) + (layer < layers - 1)
        pivots[layer] = diagonal[slot] + ends * THROUGH_CONDUCT
        right_side[layer] = base[layer] + extra[slot]

    for copy in sends:
        copy.wait_send()

    @pl.when(sub > 0)
    def _():
        to_below.wait_send()

    @pl.when(sub < subs - 1)
    def _():
        to_above.wait_send()


def finish(conc, right_side, pivots, conc_new, heat_new, sem):
    slots = conc.shape[0]
    layers = right_side.shape[0]
    writes = [
        pltpu.make_async_copy(conc.at[s], conc_new.at[0, s], sem.at[s]) for s in range(slots)
    ]
    for write in writes:
        write.start()

    def sweep(order):
        factors, values = [], []
        for layer in order:
            pivot, right = pivots[layer], right_side[layer]
            if factors:
                pivot = pivot - THROUGH_CONDUCT * factors[-1]
                right = right + THROUGH_CONDUCT * values[-1]
            inverse = 1.0 / pivot
            factors.append(THROUGH_CONDUCT * inverse)
            values.append(right * inverse)
        return factors, values

    middle = layers // 2
    low_f, low_v = sweep(range(middle))
    high_f, high_v = sweep(range(layers - 1, middle - 1, -1))
    low = (low_v[-1] + low_f[-1] * high_v[-1]) / (1.0 - low_f[-1] * high_f[-1])
    high = high_v[-1] + high_f[-1] * low
    heat_new[0, middle - 1] = low
    heat_new[0, middle] = high
    for step in range(middle - 2, -1, -1):
        low = low_v[step] + low_f[step] * low
        heat_new[0, step] = low
    for step in range(len(high_v) - 2, -1, -1):
        high = high_v[step] + high_f[step] * high
        heat_new[0, layers - 1 - step] = high
    for write in writes:
        write.wait()


def per_device(cells, subs, shell_conc, heat_rise, layer_current, layer_counts, contacts):
    _, slots, shells, gy, gx = shell_conc.shape
    _, layers, rows, _ = heat_rise.shape
    f32 = jnp.float32
    dma = pltpu.SemaphoreType.DMA
    table = (layers, rows, gx)
    held = [
        pltpu.with_memory_space_constraint(array, pltpu.HBM)
        for array in (layer_counts, contacts.T, heat_rise, shell_conc, layer_current)
    ]
    conc, right_side, pivots = pl.pallas_call(
        functools.partial(kernel, cells, subs),
        out_shape=(
            pltpu.VMEM((slots, shells, gy, gx), f32),
            pltpu.VMEM(table, f32),
            pltpu.VMEM(table, f32),
        ),
        in_specs=[
            pl.BlockSpec(memory_space=pltpu.HBM)
        ] * 5,
        out_specs=(pl.BlockSpec(memory_space=pltpu.VMEM),) * 3,
        scratch_shapes=[
            pltpu.VMEM(heat_rise.shape, f32),
            pltpu.VMEM((subs * slots, rows, gx), f32),
            pltpu.VMEM((slots, gy, gx), f32),
            pltpu.VMEM((slots, gy, gx), f32),
            pltpu.VMEM((subs * slots, rows, gx), f32),
            pltpu.VMEM((subs * slots, rows, gx), f32),
            pltpu.VMEM((layers, 1, gx), f32),
            pltpu.VMEM((layers, 1, gx), f32),
            pltpu.VMEM((cells, 2, rows, gx), f32),
            pltpu.VMEM(table, f32),
            pltpu.VMEM((subs * slots, rows, gx), f32),
            pltpu.VMEM((subs * slots, rows, gx), f32),
            pltpu.SMEM((layers,), jnp.int32),
            pltpu.SMEM(layer_counts.shape, jnp.int32),
            pltpu.SMEM(contacts.shape[::-1], jnp.int32),
            dma((7,)),
            dma((subs,)),
            dma((subs,)),
            dma((subs,)),
            dma((subs,)),
            dma((subs,)),
            dma((subs,)),
            dma((2,)),
            dma((2,)),
            dma((2 * cells,)),
            dma((2 * cells,)),
        ],
        compiler_params=pltpu.CompilerParams(
            collective_id=0, has_side_effects=True, vmem_limit_bytes=GRANT
        ),
    )(*held)
    conc_new, heat_new = pl.pallas_call(
        finish,
        out_shape=(
            jax.ShapeDtypeStruct(shell_conc.shape, f32),
            jax.ShapeDtypeStruct(heat_rise.shape, f32),
        ),
        in_specs=[pl.BlockSpec(memory_space=pltpu.VMEM)] * 3,
        out_specs=(
            pl.BlockSpec(memory_space=pl.ANY),
            pl.BlockSpec(memory_space=pltpu.VMEM),
        ),
        scratch_shapes=[dma((slots,))],
        compiler_params=pltpu.CompilerParams(vmem_limit_bytes=GRANT),
    )(conc, right_side, pivots)
    return conc_new, heat_new


def solution(mesh):
    in_specs = (
        P("cell", "sub", None, None, None),
        P("cell", None, "sub", None),
        P("cell", "sub", None, None),
        P(),
        P(),
    )
    out_specs = (P("cell", "sub", None, None, None), P("cell", None, "sub", None))
    body = functools.partial(per_device, mesh.shape["cell"], mesh.shape["sub"])
    return jax.shard_map(
        body, mesh=mesh, in_specs=in_specs, out_specs=out_specs, check_vma=False
    )
```

```python
import functools

import jax
import jax.numpy as jnp
from jax import lax
from jax.experimental import pallas as pl
from jax.experimental.pallas import tpu as pltpu
from jax.sharding import PartitionSpec as P

BASE_KELVIN = 298.15
RATE_ACTIVATION = 5000.0
DIFFUSION_ACTIVATION = 3000.0
RATE_CONSTANT = 0.5
VOLT_PER_KELVIN = 2.0 * 8.314462618 / 96485.33212
HEAT_SCALE = 10.0
ENTROPY_SLOPE = 0.001
DIFFUSION_STEP = 0.005
SURFACE_STEP = 0.005
INPLANE_CONDUCT = 0.25
THROUGH_CONDUCT = 2.0
CONTACT_CONDUCT = 0.5
MESH = pl.DeviceIdType.MESH
GRANT = 24 << 20


def partner(me, offset):
    bit = 1
    result = me
    while bit <= offset:
        if offset & bit:
            result = result + bit * (1 - 2 * ((me // bit) % 2))
        bit *= 2
    return result


def peer_of(me, offset, count):
    if count & (count - 1) == 0:
        return partner(me, offset)
    return (me + offset) % count


def inverse_sine(value):
    magnitude = jnp.abs(value)
    rooted = jnp.sqrt(1.0 + magnitude * magnitude)
    positive = jnp.log1p(magnitude + magnitude * magnitude / (1.0 + rooted))
    return jnp.where(value < 0.0, -positive, positive), rooted


def kinetics(surface, rise, current):
    kelvin = BASE_KELVIN + rise
    per_kelvin = 1.0 / kelvin
    reciprocal = rise * (1.0 / BASE_KELVIN) * per_kelvin
    ratio_rate = (
        current
        * jnp.exp(-RATE_ACTIVATION * reciprocal)
        * lax.rsqrt(surface * (1.0 - surface))
        * (0.5 / RATE_CONSTANT)
    )
    arcsine, rooted = inverse_sine(ratio_rate)
    entropic = ENTROPY_SLOPE * (0.5 - surface)
    scaled = HEAT_SCALE * current
    common = VOLT_PER_KELVIN * arcsine + entropic
    source = scaled * kelvin * common
    heat_slope = scaled * (
        common - (VOLT_PER_KELVIN * RATE_ACTIVATION) * ratio_rate * per_kelvin / rooted
    )
    return source, heat_slope


def kernel(
    cells, subs,
    counts_hbm, contacts_hbm, heat_hbm, conc, current,
    conc_in, right_side, pivots,
    heat, staged, slot_rise, current_in, surface_rows, current_rows,
    edges, low_edge, high_edge, faces, base, extra, diagonal, layer_slot, counts, contacts,
    own_sem, heat_send, heat_recv, surf_send, surf_recv, curr_send, curr_recv,
    edge_send, edge_recv, face_send, face_recv,
):
    cell = lax.axis_index("cell")
    sub = lax.axis_index("sub")
    slots, shells, gy, gx = conc_in.shape
    layers, rows, _ = heat.shape[1:]

    offsets = list(range(1, subs))
    far_first = offsets[::-1]

    def at_sub(index):
        return (cell, index)

    first_loads = [
        pltpu.make_async_copy(counts_hbm, counts, own_sem.at[5]),
        pltpu.make_async_copy(heat_hbm, heat, own_sem.at[4]),
        pltpu.make_async_copy(contacts_hbm, contacts, own_sem.at[6]),
    ]
    for load in first_loads:
        load.start()
    barrier = pltpu.get_barrier_semaphore()
    for offset in offsets:
        pl.semaphore_signal(
            barrier, inc=1, device_id=at_sub(peer_of(sub, offset, subs)), device_id_type=MESH
        )
    for offset in range(1, cells):
        pl.semaphore_signal(
            barrier, inc=1, device_id=(peer_of(cell, offset, cells), sub), device_id_type=MESH
        )

    loads = [
        pltpu.make_async_copy(current.at[0], current_in, own_sem.at[0]),
        pltpu.make_async_copy(conc.at[0], conc_in, own_sem.at[1]),
    ]
    for load in loads:
        load.start()

    for load in first_loads:
        load.wait()
    edges[0] = heat[0, :, 0]
    edges[1] = heat[0, :, rows - 1]
    start = jnp.int32(0)
    for index in range(subs):
        held = counts[index]
        for place in range(slots):
            layer = jnp.minimum(start + place, layers - 1)
            staged[index * slots + place] = heat[0, layer]
        start = start + held
    faces[cell] = jnp.zeros((2, rows, gx), jnp.float32)

    def slot_of(layer, carry):
        total = jnp.int32(0)
        slot = layer
        for index in range(subs):
            total = total + counts[index]
            slot = slot + jnp.where(total <= layer, slots - counts[index], 0)
        layer_slot[layer] = jnp.minimum(slot, subs * slots - 1)
        return carry

    pl.semaphore_wait(barrier, subs - 1 + cells - 1)

    sends = []

    def rows_of(index):
        return pl.ds(pl.multiple_of(index * rows, rows), rows)

    def slots_of(index):
        return pl.ds(index * slots, slots)

    def heat_copy(source, target, device):
        return pltpu.make_async_remote_copy(
            src_ref=staged.at[slots_of(target)],
            dst_ref=slot_rise.at[:, rows_of(source)],
            send_sem=heat_send.at[target],
            recv_sem=heat_recv.at[source],
            device_id=at_sub(device),
            device_id_type=MESH,
        )

    def surf_copy(source, target, device):
        return pltpu.make_async_remote_copy(
            src_ref=conc.at[0, :, shells - 1, rows_of(target)],
            dst_ref=surface_rows.at[slots_of(source)],
            send_sem=surf_send.at[target],
            recv_sem=surf_recv.at[source],
            device_id=at_sub(device),
            device_id_type=MESH,
        )

    def curr_copy(source, target, device):
        return pltpu.make_async_remote_copy(
            src_ref=current.at[0, :, rows_of(target)],
            dst_ref=current_rows.at[slots_of(source)],
            send_sem=curr_send.at[target],
            recv_sem=curr_recv.at[source],
            device_id=at_sub(device),
            device_id_type=MESH,
        )

    for offset in far_first:
        other = peer_of(sub, offset, subs)
        copy = heat_copy(sub, other, other)
        copy.start()
        sends.append(copy)

    for offset in far_first:
        other = peer_of(sub, offset, subs)
        for copy in (surf_copy(sub, other, other), curr_copy(sub, other, other)):
            copy.start()
            sends.append(copy)
    to_below = pltpu.make_async_remote_copy(
        src_ref=edges.at[0],
        dst_ref=high_edge,
        send_sem=edge_send.at[0],
        recv_sem=edge_recv.at[0],
        device_id=at_sub(jnp.maximum(sub - 1, 0)),
        device_id_type=MESH,
    )
    to_above = pltpu.make_async_remote_copy(
        src_ref=edges.at[1],
        dst_ref=low_edge,
        send_sem=edge_send.at[1],
        recv_sem=edge_recv.at[1],
        device_id=at_sub(jnp.minimum(sub + 1, subs - 1)),
        device_id_type=MESH,
    )

    @pl.when(sub > 0)
    def _():
        to_below.start()

    @pl.when(sub < subs - 1)
    def _():
        to_above.start()

    def face_copies(source, device):
        return [
            pltpu.make_async_remote_copy(
                src_ref=heat_hbm.at[0, layer],
                dst_ref=faces.at[source, place],
                send_sem=face_send.at[2 * device + place],
                recv_sem=face_recv.at[2 * source + place],
                device_id=(device, sub),
                device_id_type=MESH,
            )
            for place, layer in ((0, 0), (1, layers - 1))
        ]

    for offset in range(1, cells):
        for copy in face_copies(cell, peer_of(cell, offset, cells)):
            copy.start()
            sends.append(copy)

    mine = [
        pltpu.make_async_copy(
            conc.at[0, :, shells - 1, rows_of(sub)], surface_rows.at[slots_of(sub)], own_sem.at[2]
        ),
        pltpu.make_async_copy(
            current.at[0, :, rows_of(sub)], current_rows.at[slots_of(sub)], own_sem.at[3]
        ),
    ]
    for copy in mine:
        copy.start()
    slot_rise[:, rows_of(sub)] = staged[slots_of(sub)]

    lax.fori_loop(0, layers, slot_of, jnp.int32(0))

    live_count = counts[sub]
    live = lax.broadcasted_iota(jnp.int32, (slots, rows, gx), 0) < live_count
    volumes = [((r + 1) ** 3 - r**3) / (3.0 * shells**3) for r in range(shells)]
    weights = [DIFFUSION_STEP * ((r + 1) ** 2 / shells**2 * shells) for r in range(shells - 1)]

    def particle(where):
        rise = slot_rise[:, where]
        speedup = jnp.exp(
            (DIFFUSION_ACTIVATION / BASE_KELVIN) * rise / (BASE_KELVIN + rise)
        )
        uppers = []
        values = []
        link = None
        for r in range(shells):
            right = volumes[r] * conc_in[:, r, where]
            if r == shells - 1:
                right = right - SURFACE_STEP * current_in[:, where]
            pivot = volumes[r]
            if r > 0:
                pivot = pivot + link * (1.0 - uppers[r - 1])
                right = right + link * values[r - 1]
            if r < shells - 1:
                next_link = weights[r] * speedup
                pivot = pivot + next_link
            inverse = 1.0 / pivot
            if r < shells - 1:
                uppers.append(next_link * inverse)
                link = next_link
            values.append(right * inverse)
        result = values[shells - 1]
        conc_in[:, shells - 1, where] = jnp.where(live, result, 0.0)
        for r in range(shells - 2, -1, -1):
            result = values[r] + uppers[r] * result
            conc_in[:, r, where] = jnp.where(live, result, 0.0)

    for load in loads:
        load.wait()
    for offset in [0] + offsets:
        other = peer_of(sub, offset, subs)
        if offset:
            heat_copy(other, sub, other).wait_recv()
        particle(rows_of(other))

    @pl.when(sub > 0)
    def _():
        to_above.wait_recv()

    @pl.when(sub == 0)
    def _():
        low_edge[...] = edges[0]

    @pl.when(sub < subs - 1)
    def _():
        to_below.wait_recv()

    @pl.when(sub == subs - 1)
    def _():
        high_edge[...] = edges[1]

    for offset in range(1, cells):
        other = peer_of(cell, offset, cells)
        for copy in face_copies(other, other):
            copy.wait_recv()

    row_index = lax.broadcasted_iota(jnp.int32, (rows, gx), 0)
    lane_index = lax.broadcasted_iota(jnp.int32, (rows, gx), 1)

    def fill(layer, carry):
        here = heat[0, layer]
        up = pltpu.roll(here, 1, 0)
        up = jnp.where(row_index == 0, low_edge[pl.ds(layer, 1)], up)
        down = pltpu.roll(here, rows - 1, 0)
        down = jnp.where(row_index == rows - 1, high_edge[pl.ds(layer, 1)], down)
        left = jnp.where(lane_index == 0, here, pltpu.roll(here, 1, 1))
        right = jnp.where(lane_index == gx - 1, here, pltpu.roll(here, gx - 1, 1))
        laplace = down + up + right + left - 4.0 * here
        base[layer] = here + INPLANE_CONDUCT * laplace
        return carry

    lax.fori_loop(0, layers, fill, jnp.int32(0), unroll=2)
    lower = contacts[0, cell]
    upper = contacts[1, cell]
    below_face = jnp.where(lower >= 0, faces[jnp.maximum(lower, 0), 1], 0.0)
    above_face = jnp.where(upper >= 0, faces[jnp.maximum(upper, 0), 0], 0.0)
    base[0] = base[0] + CONTACT_CONDUCT * (below_face - heat[0, 0])
    base[layers - 1] = base[layers - 1] + CONTACT_CONDUCT * (above_face - heat[0, layers - 1])

    for offset in [0] + far_first:
        other = peer_of(sub, offset, subs)
        if offset:
            surf_copy(other, sub, other).wait_recv()
            curr_copy(other, sub, other).wait_recv()
        else:
            for copy in mine:
                copy.wait()
        at = slots_of(other)
        rise = staged[at]
        source, slope = kinetics(surface_rows[at], rise, current_rows[at])
        extra[at] = source - slope * rise
        diagonal[at] = 1.0 - slope

    for layer in range(layers):
        slot = layer_slot[layer]
        ends = (layer > 0) + (layer < layers - 1)
        pivots[layer] = diagonal[slot] + ends * THROUGH_CONDUCT
        right_side[layer] = base[layer] + extra[slot]

    for copy in sends:
        copy.wait_send()

    @pl.when(sub > 0)
    def _():
        to_below.wait_send()

    @pl.when(sub < subs - 1)
    def _():
        to_above.wait_send()


def finish(conc, right_side, pivots, conc_new, heat_new, sem):
    slots = conc.shape[0]
    layers = right_side.shape[0]
    writes = [
        pltpu.make_async_copy(conc.at[s], conc_new.at[0, s], sem.at[s]) for s in range(slots)
    ]
    for write in writes:
        write.start()

    def sweep(order):
        factors, values = [], []
        for layer in order:
            pivot, right = pivots[layer], right_side[layer]
            if factors:
                pivot = pivot - THROUGH_CONDUCT * factors[-1]
                right = right + THROUGH_CONDUCT * values[-1]
            inverse = 1.0 / pivot
            factors.append(THROUGH_CONDUCT * inverse)
            values.append(right * inverse)
        return factors, values

    middle = layers // 2
    low_f, low_v = sweep(range(middle))
    high_f, high_v = sweep(range(layers - 1, middle - 1, -1))
    low = (low_v[-1] + low_f[-1] * high_v[-1]) / (1.0 - low_f[-1] * high_f[-1])
    high = high_v[-1] + high_f[-1] * low
    heat_new[0, middle - 1] = low
    heat_new[0, middle] = high
    for step in range(middle - 2, -1, -1):
        low = low_v[step] + low_f[step] * low
        heat_new[0, step] = low
    for step in range(len(high_v) - 2, -1, -1):
        high = high_v[step] + high_f[step] * high
        heat_new[0, layers - 1 - step] = high
    for write in writes:
        write.wait()


def per_device(cells, subs, shell_conc, heat_rise, layer_current, layer_counts, contacts):
    _, slots, shells, gy, gx = shell_conc.shape
    _, layers, rows, _ = heat_rise.shape
    f32 = jnp.float32
    dma = pltpu.SemaphoreType.DMA
    table = (layers, rows, gx)
    held = [
        pltpu.with_memory_space_constraint(array, pltpu.HBM)
        for array in (layer_counts, contacts.T, heat_rise, shell_conc, layer_current)
    ]
    conc, right_side, pivots = pl.pallas_call(
        functools.partial(kernel, cells, subs),
        out_shape=(
            pltpu.VMEM((slots, shells, gy, gx), f32),
            pltpu.VMEM(table, f32),
            pltpu.VMEM(table, f32),
        ),
        in_specs=[
            pl.BlockSpec(memory_space=pltpu.HBM)
        ] * 5,
        out_specs=(pl.BlockSpec(memory_space=pltpu.VMEM),) * 3,
        scratch_shapes=[
            pltpu.VMEM(heat_rise.shape, f32),
            pltpu.VMEM((subs * slots, rows, gx), f32),
            pltpu.VMEM((slots, gy, gx), f32),
            pltpu.VMEM((slots, gy, gx), f32),
            pltpu.VMEM((subs * slots, rows, gx), f32),
            pltpu.VMEM((subs * slots, rows, gx), f32),
            pltpu.VMEM((2, layers, gx), f32),
            pltpu.VMEM((layers, gx), f32),
            pltpu.VMEM((layers, gx), f32),
            pltpu.VMEM((cells, 2, rows, gx), f32),
            pltpu.VMEM(table, f32),
            pltpu.VMEM((subs * slots, rows, gx), f32),
            pltpu.VMEM((subs * slots, rows, gx), f32),
            pltpu.SMEM((layers,), jnp.int32),
            pltpu.SMEM(layer_counts.shape, jnp.int32),
            pltpu.SMEM(contacts.shape[::-1], jnp.int32),
            dma((7,)),
            dma((subs,)),
            dma((subs,)),
            dma((subs,)),
            dma((subs,)),
            dma((subs,)),
            dma((subs,)),
            dma((2,)),
            dma((2,)),
            dma((2 * cells,)),
            dma((2 * cells,)),
        ],
        compiler_params=pltpu.CompilerParams(
            collective_id=0, has_side_effects=True, vmem_limit_bytes=GRANT
        ),
    )(*held)
    conc_new, heat_new = pl.pallas_call(
        finish,
        out_shape=(
            jax.ShapeDtypeStruct(shell_conc.shape, f32),
            jax.ShapeDtypeStruct(heat_rise.shape, f32),
        ),
        in_specs=[pl.BlockSpec(memory_space=pltpu.VMEM)] * 3,
        out_specs=(
            pl.BlockSpec(memory_space=pl.ANY),
            pl.BlockSpec(memory_space=pltpu.VMEM),
        ),
        scratch_shapes=[dma((slots,))],
        compiler_params=pltpu.CompilerParams(vmem_limit_bytes=GRANT),
    )(conc, right_side, pivots)
    return conc_new, heat_new


def solution(mesh):
    in_specs = (
        P("cell", "sub", None, None, None),
        P("cell", None, "sub", None),
        P("cell", "sub", None, None),
        P(),
        P(),
    )
    out_specs = (P("cell", "sub", None, None, None), P("cell", None, "sub", None))
    body = functools.partial(per_device, mesh.shape["cell"], mesh.shape["sub"])
    return jax.shard_map(
        body, mesh=mesh, in_specs=in_specs, out_specs=out_specs, check_vma=False
    )
```
